512 devices in a mesh: space: 128 (over x, z_hi, y, core), cols: 4 (over z_lo).
Axes of the slice: x: 4, y: 8, z: 8 (z_hi: 2, z_lo: 4; z = z_hi * 4 + z_lo), core: 2. Of those that a mesh axis runs over, the one named last changes fastest.
Arguments:
- propagator: float32 [2, 65536, 1024], P(None, 'space', 'cols'), may hold values from -6 to 6
- couplings: float32 [4, 512, 8, 128, 128], P('cols', 'space'), may hold values from -0.1875 to 0.1875
- frame_energies: float32 [4, 65536], P('cols', 'space'), may hold values from -6 to 6
- block_lists: int32 [4, 512, 8], P('cols', 'space'), may hold values from 0 to 511, as said below
- frame_owner: int32 [1], replicated, may hold values from 0 to 65535
Outputs:
- advanced: float32 [2, 65536, 1024], P(None, 'space', 'cols')
The draws below stay inside these ranges and needn't reach their ends.
Inputs may be any that keep to these rules, and one draw needn't show every extreme that they name: `block_lists`: for every frame and block row g, entry 0 is g itself and the other entries are (g + o) mod 512 for 7 different nonzero o between -4 and 4.
All inputs are finite; a program needn't handle non-finite values.
Results may differ from the reference program's by a relative error of at most 0.00005.
Values sent between devices are 32-bit elements; how exact they have to be, the bound alone decides.
A program may use at most 64 MiB of HBM per device.

```python
import jax
import jax.numpy as jnp
from jax import lax

BLOCK = 128
REACH = 4
WIDTH = 8
NBLK = 512
OSC = 65536
WINDOW = 1024
FRAMES = 4


def draw_block_lists(key, part):
    nonzero = jnp.concatenate([jnp.arange(-REACH, 0), jnp.arange(1, REACH + 1)]).astype(jnp.int32)
    dropped = jax.random.randint(key, (FRAMES, NBLK, 1), 0, 2 * REACH).astype(jnp.int32)
    slots = jnp.arange(2 * REACH - 1, dtype=jnp.int32)[None, None, :]
    picks = slots + (slots >= dropped).astype(jnp.int32)
    offsets = nonzero[picks]
    offsets = jnp.concatenate([jnp.zeros((FRAMES, NBLK, 1), jnp.int32), offsets], axis=2)
    row_blocks = jnp.arange(NBLK, dtype=jnp.int32)[None, :, None]
    return jnp.mod(row_blocks + offsets, NBLK).astype(jnp.int32)


def block_scale(stream_key, extent, pieces, low, largest):
    loudness = 1.0
    for dim, blocks in pieces:
        heights = jax.random.uniform(jax.random.fold_in(jax.random.fold_in(stream_key, 6), dim), (blocks,), jnp.float32, low / len(pieces), largest / len(pieces))
        loudness = loudness * jnp.repeat(jnp.exp(heights), extent[dim] // blocks).reshape((-1,) + (1,) * (len(extent) - 1 - dim))
    return loudness


def gaussian(key, extent, deviation, bound, split=(), held_as=jnp.bfloat16):
    drawn = deviation * jax.random.normal(key, extent, jnp.float32)
    if split:
        drawn = drawn * block_scale(key, extent, split, -0.22, 0.18)
    return jnp.clip(drawn, -bound, bound).astype(held_as)


def setup_inputs(seed: int = 0) -> dict:
    key_list = jax.random.split(jax.random.key(seed), 6)
    return {
        "propagator": gaussian(key_list[0], (2, OSC, WINDOW), 1.0, 6.0, ((1, 128), (2, 4)), jnp.float32),
        "couplings": gaussian(key_list[1], (FRAMES, NBLK, WIDTH, BLOCK, BLOCK), (WIDTH * BLOCK) ** -0.5, 0.1875, ((0, 4), (1, 128)), jnp.float32),
        "frame_energies": gaussian(key_list[2], (FRAMES, OSC), 1.0, 6.0, ((0, 4), (1, 128)), jnp.float32),
        "block_lists": draw_block_lists(jax.random.fold_in(key_list[5], 71), 0),
        "frame_owner": jax.random.randint(key_list[4], (1,), 0, 65536).astype(jnp.int32),
    }


bessel_zero = 0.7651976865579666
bessel_one = 0.44005058574493355
bessel_two = 0.11490348493190049
spectral_scale = 8.0
phase_unit = 6.283185307179586 / 97.0


def apply_scaled(field, coupling, energies, lists):
    total_blocks = lists.shape[0]
    block = coupling.shape[2]
    window = field.shape[2]
    blocks = field.reshape(2, total_blocks, block, window)

    def one_block(row_block):
        picked = blocks[:, lists[row_block]]
        product = jnp.einsum("kij,ckjw->ciw", coupling[row_block], picked, precision=lax.Precision.HIGHEST)
        own_rows = lax.dynamic_index_in_dim(blocks, row_block, 1, keepdims=False)
        local_energy = lax.dynamic_slice_in_dim(energies, row_block * block, block)
        return product + local_energy[None, :, None] * own_rows

    result = lax.map(one_block, jnp.arange(total_blocks, dtype=jnp.int32))
    return jnp.transpose(result, (1, 0, 2, 3)).reshape(2, total_blocks * block, window) / spectral_scale


def reference(propagator, couplings, frame_energies, block_lists, frame_owner):
    moment = frame_owner[0]
    owner = jnp.mod(moment, FRAMES).astype(jnp.int32)
    turn = jnp.mod(moment // FRAMES, 97).astype(jnp.int32)
    coupling = couplings[owner]
    energies = frame_energies[owner]
    lists = block_lists[owner]
    first_term = apply_scaled(propagator, coupling, energies, lists)
    second_term = 2.0 * apply_scaled(first_term, coupling, energies, lists) - propagator
    real_part = bessel_zero * propagator[0] + 2.0 * bessel_one * first_term[1] - 2.0 * bessel_two * second_term[0]
    imag_part = bessel_zero * propagator[1] - 2.0 * bessel_one * first_term[0] - 2.0 * bessel_two * second_term[1]
    angle = turn.astype(jnp.float32) * phase_unit
    cosine = jnp.cos(angle)
    sine = jnp.sin(angle)
    return jnp.stack([cosine * real_part + sine * imag_part, cosine * imag_part - sine * real_part])
```

```python
import functools

import jax
import jax.numpy as jnp
from jax import lax
from jax.experimental import pallas as pl
from jax.experimental.pallas import tpu as pltpu
from jax.sharding import PartitionSpec as P

REACH = 4
MESH = pl.DeviceIdType.MESH

bessel_zero = 0.7651976865579666
bessel_one = 0.44005058574493355
bessel_two = 0.11490348493190049
phase_unit = 6.283185307179586 / 97.0


def halves(value):
    high = value.astype(jnp.bfloat16)
    low = (value - high.astype(jnp.float32)).astype(jnp.bfloat16)
    return high, low


def step_kernel(
    owner, ring, line, blocks, width, block, window,
    phase, energies, index, field, coupling, out,
    vext, wext, vhalf, whalf, cbuf, chigh, clow, ebuf, ibuf, slots,
    halo_send, halo_recv, own_sem, next_send, next_recv, couple_send, couple_recv,
    energy_send, energy_recv, index_send, index_recv, slot_sem,
):
    space = lax.axis_index("space")
    col = lax.axis_index("cols")
    right = lax.rem(space + 1, ring)
    left = lax.rem(space + ring - 1, ring)
    pieces = cbuf.shape[0]
    per_row = pieces // blocks
    pair = width // per_row

    barrier = pltpu.get_barrier_semaphore()
    pl.semaphore_signal(barrier, inc=1, device_id=(left, col), device_id_type=MESH)
    pl.semaphore_signal(barrier, inc=1, device_id=(right, col), device_id_type=MESH)

    @pl.when(col > 0)
    def _():
        pl.semaphore_signal(barrier, inc=1, device_id=(space, col - 1), device_id_type=MESH)

    @pl.when(col < line - 1)
    def _():
        pl.semaphore_signal(barrier, inc=1, device_id=(space, col + 1), device_id_type=MESH)

    @pl.when((col > 0) & (col < line - 1))
    def _():
        pl.semaphore_wait(barrier, 4)

    @pl.when((col == 0) | (col == line - 1))
    def _():
        pl.semaphore_wait(barrier, 3)

    is_owner = col == owner
    go_up = (col >= owner) & (col < line - 1)
    go_down = (col <= owner) & (col > 0)

    def hop(way, source, target, send_sem, recv_sem):
        to = col + 1 if way == 0 else col - 1
        return pltpu.make_async_remote_copy(
            src_ref=source, dst_ref=target, send_sem=send_sem, recv_sem=recv_sem,
            device_id=(space, to), device_id_type=MESH,
        )

    def piece_hop(way, source, i):
        return hop(way, source.at[i], cbuf.at[i], couple_send.at[way, i], couple_recv.at[i])

    def energy_hop(way, source):
        return hop(way, source, ebuf, energy_send.at[way], energy_recv)

    def index_hop(way, source):
        return hop(way, source, ibuf, index_send.at[way], index_recv)

    both = ((0, go_up), (1, go_down))

    @pl.when(is_owner)
    def _():
        for way, go in both:
            @pl.when(go)
            def _():
                index_hop(way, index).start()
                energy_hop(way, energies).start()
        pltpu.make_async_copy(index, ibuf, index_recv).start()
        pltpu.make_async_copy(energies, ebuf, energy_recv).start()

        def send_piece(i, carry):
            for way, go in both:
                @pl.when(go)
                def _():
                    piece_hop(way, coupling, i).start()
            pltpu.make_async_copy(coupling.at[i], cbuf.at[i], couple_recv.at[i]).start()
            return carry

        lax.fori_loop(0, pieces, send_piece, 0)

    def halo_copy(side):
        to, at = ((right, 0), (left, 2 * blocks))[side]
        return pltpu.make_async_remote_copy(
            src_ref=field, dst_ref=vext.at[:, pl.ds(at, blocks)],
            send_sem=halo_send.at[side], recv_sem=halo_recv.at[side],
            device_id=(to, col), device_id_type=MESH,
        )

    halo_copy(0).start()
    halo_copy(1).start()
    own = pltpu.make_async_copy(field, vext.at[:, pl.ds(blocks, blocks)], own_sem)
    own.start()

    pltpu.make_async_copy(ibuf, ibuf, index_recv).wait()
    pltpu.make_async_copy(ebuf, ebuf, energy_recv).wait()

    @pl.when(jnp.logical_not(is_owner))
    def _():
        for way, go in both:
            @pl.when(go)
            def _():
                index_hop(way, ibuf).start()
                energy_hop(way, ebuf).start()

    to_slots = pltpu.make_async_copy(ibuf, slots, slot_sem)
    to_slots.start()

    def take_pieces(first_piece, last_piece):
        def take(i, carry):
            pltpu.make_async_copy(cbuf.at[i], cbuf.at[i], couple_recv.at[i]).wait()

            @pl.when(jnp.logical_not(is_owner))
            def _():
                for way, go in both:
                    @pl.when(go)
                    def _():
                        piece_hop(way, cbuf, i).start()
            return carry

        lax.fori_loop(first_piece, last_piece, take, 0)

    def split_into(target, at, re, im):
        re_high, re_low = halves(re)
        im_high, im_low = halves(im)
        target[at, 0, :, 0:window] = re_high
        target[at, 0, :, window:] = im_high
        target[at, 1, :, 0:window] = re_low
        target[at, 1, :, window:] = im_low

    def product(r, source):
        total = [jnp.zeros((block, window), jnp.float32) for _ in range(2)]
        for k in range(0, width, 2):
            e0 = slots[0, r * width + k]
            e1 = slots[0, r * width + k + 1]
            lanes = pl.ds(k * block, 2 * block)
            high = chigh[r, :, lanes]
            low = clow[r, :, lanes]
            for part in range(2):
                span = pl.ds(part * window, window)
                v_high = jnp.concatenate([source[e0, 0, :, span], source[e1, 0, :, span]], axis=0)
                v_low = jnp.concatenate([source[e0, 1, :, span], source[e1, 1, :, span]], axis=0)
                total[part] += jnp.dot(high, v_high, preferred_element_type=jnp.float32)
                total[part] += jnp.dot(low, v_high, preferred_element_type=jnp.float32)
                total[part] += jnp.dot(high, v_low, preferred_element_type=jnp.float32)
        return total[0] * 0.125, total[1] * 0.125

    def next_copy(side, r):
        to, at = ((right, r), (left, 2 * blocks + r))[side]
        return pltpu.make_async_remote_copy(
            src_ref=wext.at[:, blocks + r], dst_ref=wext.at[:, at],
            send_sem=next_send.at[side, r], recv_sem=next_recv.at[side, r],
            device_id=(to, col), device_id_type=MESH,
        )

    def first_row(r, carry):
        on_diagonal = lax.broadcasted_iota(jnp.int32, (block, block), 0) == lax.broadcasted_iota(
            jnp.int32, (block, block), 1
        )
        level = jnp.broadcast_to(ebuf[pl.ds(r, 1), :], (block, block))
        for k in range(width):
            value = cbuf[r * per_row + k // pair, k % pair]
            if k == 0:
                value = value + jnp.where(on_diagonal, level, 0.0)
            high, low = halves(value)
            chigh[r, :, k * block : (k + 1) * block] = high
            clow[r, :, k * block : (k + 1) * block] = low
        re, im = product(r, vhalf)
        wext[0, blocks + r] = re
        wext[1, blocks + r] = im
        split_into(whalf, blocks + r, re, im)
        next_copy(0, r).start()
        next_copy(1, r).start()
        return carry

    early = (blocks - 1) * per_row
    take_pieces(0, early)
    own.wait()
    halo_copy(0).wait()
    halo_copy(1).wait()
    to_slots.wait()

    def split_field(e, carry):
        split_into(vhalf, e, vext[0, e], vext[1, e])
        return carry

    lax.fori_loop(0, 3 * blocks, split_field, 0)
    lax.fori_loop(0, blocks - 1, first_row, 0)
    take_pieces(early, pieces)
    first_row(blocks - 1, 0)

    def split_next(r, carry):
        next_copy(0, r).wait()
        next_copy(1, r).wait()
        split_into(whalf, r, wext[0, r], wext[1, r])
        split_into(whalf, 2 * blocks + r, wext[0, 2 * blocks + r], wext[1, 2 * blocks + r])
        return carry

    lax.fori_loop(0, blocks, split_next, 0)
    cosine = phase[0]
    sine = phase[1]

    def last_row(r, carry):
        re, im = product(r, whalf)
        keep = bessel_zero + 2.0 * bessel_two
        u_re = keep * vext[0, blocks + r] + 2.0 * bessel_one * wext[1, blocks + r] - 4.0 * bessel_two * re
        u_im = keep * vext[1, blocks + r] - 2.0 * bessel_one * wext[0, blocks + r] - 4.0 * bessel_two * im
        out[0, r] = cosine * u_re + sine * u_im
        out[1, r] = cosine * u_im - sine * u_re
        return carry

    lax.fori_loop(0, blocks, last_row, 0)

    for way, go in both:
        @pl.when(go)
        def _():
            index_hop(way, ibuf).wait_send()
            energy_hop(way, ebuf).wait_send()

            def drain(i, carry):
                piece_hop(way, cbuf, i).wait_send()
                return carry

            lax.fori_loop(0, pieces, drain, 0)


def per_device(propagator, couplings, frame_energies, block_lists, frame_owner):
    line = lax.axis_size("cols")
    ring = lax.axis_size("space")
    moment = frame_owner[0]
    owner = jnp.mod(moment, line)
    turn = jnp.mod(moment // line, 97)
    _, blocks, width, block, _ = couplings.shape
    window = propagator.shape[2]
    angle = turn.astype(jnp.float32) * phase_unit
    phase = jnp.stack([jnp.cos(angle), jnp.sin(angle)])
    total_blocks = blocks * ring
    first_block = lax.axis_index("space") * blocks
    index = jnp.mod(block_lists[0] - first_block + REACH, total_blocks).astype(jnp.int32)
    index = jnp.pad(index.reshape(1, blocks * width), ((0, 7), (0, 128 - blocks * width)))
    energies = frame_energies.reshape(blocks, block)
    field = propagator.reshape(2, blocks, block, window)
    pieces = blocks * width // 2
    coupling = couplings.reshape(pieces, 2, block, block)

    def call(which):
        anywhere = pl.BlockSpec(memory_space=pl.ANY)
        dma = pltpu.SemaphoreType.DMA
        return pl.pallas_call(
            functools.partial(step_kernel, which, ring, line, blocks, width, block, window),
            out_shape=jax.ShapeDtypeStruct((2, blocks, block, window), jnp.float32),
            in_specs=[pl.BlockSpec(memory_space=pltpu.SMEM)] + [anywhere] * 4,
            out_specs=pl.BlockSpec(memory_space=pltpu.VMEM),
            scratch_shapes=[
                pltpu.VMEM((2, 3 * blocks, block, window), jnp.float32),
                pltpu.VMEM((2, 3 * blocks, block, window), jnp.float32),
                pltpu.VMEM((3 * blocks, 2, block, 2 * window), jnp.bfloat16),
                pltpu.VMEM((3 * blocks, 2, block, 2 * window), jnp.bfloat16),
                pltpu.VMEM((pieces, 2, block, block), jnp.float32),
                pltpu.VMEM((blocks, block, width * block), jnp.bfloat16),
                pltpu.VMEM((blocks, block, width * block), jnp.bfloat16),
                pltpu.VMEM((blocks, block), jnp.float32),
                pltpu.VMEM((8, 128), jnp.int32),
                pltpu.SMEM((8, 128), jnp.int32),
                dma((2,)), dma((2,)), dma,
                dma((2, blocks)), dma((2, blocks)),
                dma((2, pieces)), dma((pieces,)),
                dma((2,)), dma, dma((2,)), dma, dma,
            ],
            compiler_params=pltpu.CompilerParams(
                collective_id=which, has_side_effects=True, vmem_limit_bytes=48 << 20
            ),
            name="step",
        )

    branches = [call(which) for which in range(line)]
    result = lax.switch(owner, branches, phase, energies, index, field, coupling)
    return result.reshape(2, blocks * block, window)


def solution(mesh):
    in_specs = (
        P(None, "space", "cols"),
        P("cols", "space", None, None, None),
        P("cols", "space"),
        P("cols", "space", None),
        P(),
    )
    out_specs = P(None, "space", "cols")
    return jax.shard_map(
        per_device, mesh=mesh, in_specs=in_specs, out_specs=out_specs, check_vma=False
    )
```

```python
import functools

import jax
import jax.numpy as jnp
from jax import lax
from jax.experimental import pallas as pl
from jax.experimental.pallas import tpu as pltpu
from jax.sharding import PartitionSpec as P

REACH = 4
PLACE = (4, 2, 8, 2)
MESH = pl.DeviceIdType.MESH

bessel_zero = 0.7651976865579666
bessel_one = 0.44005058574493355
bessel_two = 0.11490348493190049
phase_unit = 6.283185307179586 / 97.0


def halves(value):
    high = value.astype(jnp.bfloat16)
    low = (value - high.astype(jnp.float32)).astype(jnp.bfloat16)
    return high, low


def step_kernel(
    owner, ring, line, blocks, width, block, window,
    phase, energies, index, field, coupling, out,
    vext, wext, vhalf, whalf, cbuf, chigh, clow, ebuf, ibuf, slots,
    halo_send, halo_recv, own_sem, next_send, next_recv, couple_send, couple_recv,
    energy_send, energy_recv, index_send, index_recv, slot_sem,
    rbuf, sbuf, relay_send, relay_recv, relay_next_send, relay_next_recv,
):
    space = lax.axis_index("space")
    col = lax.axis_index("cols")
    right = lax.rem(space + 1, ring)
    left = lax.rem(space + ring - 1, ring)
    pieces = cbuf.shape[0]
    per_row = pieces // blocks
    pair = width // per_row

    xs, zhs, ys, cores = PLACE
    zs = zhs * line
    core = lax.rem(space, cores)
    y = lax.rem(lax.div(space, cores), ys)
    z_hi = lax.rem(lax.div(space, cores * ys), zhs)
    x = lax.div(space, cores * ys * zhs)
    z = z_hi * line + col
    quarter = zs // 4

    def around(value, count):
        return lax.rem(value + count, count)

    def device(at_x, at_y, at_z, at_core):
        run = around(at_x, xs) * zhs + lax.div(at_z, line)
        return (run * ys + at_y) * cores + at_core, lax.rem(at_z, line)

    is_last = (y == ys - 1) & (core == cores - 1)
    is_first = (y == 0) & (core == 0)
    relays_up = y == 1
    relays_down = y == ys - 2
    relays = relays_up | relays_down
    x_after = x + z_hi
    x_before = x - (1 - z_hi)
    z_far = (around(z + quarter, zs), around(z - quarter, zs))
    up_relay = [device(x_after, 1, z_far[part], part) for part in range(2)]
    up_relay_in = [device(x, 1, z_far[1 - part], part) for part in range(2)]
    down_relay = [device(x_before, ys - 2, z_far[part], part) for part in range(2)]
    down_relay_in = [device(x, ys - 2, z_far[1 - part], part) for part in range(2)]
    z_from = around(z - quarter + 2 * quarter * core, zs)
    z_to = around(z_from + 2 * quarter, zs)
    up_from = device(x - lax.div(z_from, line), ys - 1, z_from, cores - 1)
    up_to = device(x, 0, z_to, 0)
    down_from = device(x + lax.div(z_to, line), 0, z_from, 0)
    down_to = device(x, ys - 1, z_to, cores - 1)

    barrier = pltpu.get_barrier_semaphore()

    def greet(*others):
        for other in others:
            pl.semaphore_signal(barrier, inc=1, device_id=other, device_id_type=MESH)

    @pl.when(jnp.logical_not(is_first))
    def _():
        greet((left, col))

    @pl.when(jnp.logical_not(is_last))
    def _():
        greet((right, col))

    @pl.when(is_last)
    def _():
        greet(*up_relay, *down_relay_in)

    @pl.when(is_first)
    def _():
        greet(*down_relay, *up_relay_in)

    @pl.when(relays_up)
    def _():
        greet(up_from, up_to)

    @pl.when(relays_down)
    def _():
        greet(down_from, down_to)

    @pl.when(col > 0)
    def _():
        greet((space, col - 1))

    @pl.when(col < line - 1)
    def _():
        greet((space, col + 1))

    greeters = (
        3
        + jnp.where((col > 0) & (col < line - 1), 1, 0)
        + jnp.where(is_first | is_last, 3, 0)
        + jnp.where(relays, 2, 0)
    )
    pl.semaphore_wait(barrier, greeters)

    is_owner = col == owner
    go_up = (col >= owner) & (col < line - 1)
    go_down = (col <= owner) & (col > 0)

    def hop(way, source, target, send_sem, recv_sem):
        to = col + 1 if way == 0 else col - 1
        return pltpu.make_async_remote_copy(
            src_ref=source, dst_ref=target, send_sem=send_sem, recv_sem=recv_sem,
            device_id=(space, to), device_id_type=MESH,
        )

    def piece_hop(way, source, i):
        return hop(way, source.at[i], cbuf.at[i], couple_send.at[way, i], couple_recv.at[i])

    def energy_hop(way, source):
        return hop(way, source, ebuf, energy_send.at[way], energy_recv)

    def index_hop(way, source):
        return hop(way, source, ibuf, index_send.at[way], index_recv)

    both = ((0, go_up), (1, go_down))

    @pl.when(is_owner)
    def _():
        for way, go in both:
            @pl.when(go)
            def _():
                index_hop(way, index).start()
                energy_hop(way, energies).start()
        pltpu.make_async_copy(index, ibuf, index_recv).start()
        pltpu.make_async_copy(energies, ebuf, energy_recv).start()

        def send_piece(i, carry):
            for way, go in both:
                @pl.when(go)
                def _():
                    piece_hop(way, coupling, i).start()
            pltpu.make_async_copy(coupling.at[i], cbuf.at[i], couple_recv.at[i]).start()
            return carry

        lax.fori_loop(0, pieces, send_piece, 0)

    low_at, high_at = 0, 2 * blocks

    def push(source, target, send_sem, recv_sem, to):
        return pltpu.make_async_remote_copy(
            src_ref=source, dst_ref=target, send_sem=send_sem, recv_sem=recv_sem,
            device_id=to, device_id_type=MESH,
        )

    def halo_copy(side, part):
        to, at = ((right, low_at), (left, high_at))[side]
        return push(
            field.at[part], vext.at[part, pl.ds(at, blocks)],
            halo_send.at[side, part], halo_recv.at[side, part], (to, col),
        )

    def halo_start(side):
        edge, via = ((is_last, up_relay), (is_first, down_relay))[side]

        @pl.when(edge)
        def _():
            for part in range(2):
                push(field.at[part], rbuf, halo_send.at[side, part], relay_recv, via[part]).start()

        @pl.when(jnp.logical_not(edge))
        def _():
            for part in range(2):
                halo_copy(side, part).start()

    roles = ((0, low_at, relays_up, up_to), (1, high_at, relays_down, down_to))

    def relay_halo():
        for side, at, role, to in roles:
            @pl.when(role)
            def _():
                passed = push(
                    rbuf, vext.at[core, pl.ds(at, blocks)], relay_send, halo_recv.at[side, core], to
                )
                pltpu.make_async_copy(rbuf, rbuf, relay_recv).wait()
                passed.start()

    halo_start(0)
    halo_start(1)
    own = pltpu.make_async_copy(field, vext.at[:, pl.ds(blocks, blocks)], own_sem)
    own.start()

    pltpu.make_async_copy(ibuf, ibuf, index_recv).wait()
    pltpu.make_async_copy(ebuf, ebuf, energy_recv).wait()

    @pl.when(jnp.logical_not(is_owner))
    def _():
        for way, go in both:
            @pl.when(go)
            def _():
                index_hop(way, ibuf).start()
                energy_hop(way, ebuf).start()

    to_slots = pltpu.make_async_copy(ibuf, slots, slot_sem)
    to_slots.start()

    def take_pieces(first_piece, last_piece):
        def take(i, carry):
            pltpu.make_async_copy(cbuf.at[i], cbuf.at[i], couple_recv.at[i]).wait()

            @pl.when(jnp.logical_not(is_owner))
            def _():
                for way, go in both:
                    @pl.when(go)
                    def _():
                        piece_hop(way, cbuf, i).start()
            return carry

        lax.fori_loop(first_piece, last_piece, take, 0)

    def split_into(target, at, re, im):
        re_high, re_low = halves(re)
        im_high, im_low = halves(im)
        target[at, 0, :, 0:window] = re_high
        target[at, 0, :, window:] = im_high
        target[at, 1, :, 0:window] = re_low
        target[at, 1, :, window:] = im_low

    def product(r, source):
        total = [jnp.zeros((block, window), jnp.float32) for _ in range(2)]
        for k in range(0, width, 2):
            e0 = slots[0, r * width + k]
            e1 = slots[0, r * width + k + 1]
            lanes = pl.ds(k * block, 2 * block)
            high = chigh[r, :, lanes]
            low = clow[r, :, lanes]
            for part in range(2):
                span = pl.ds(part * window, window)
                v_high = jnp.concatenate([source[e0, 0, :, span], source[e1, 0, :, span]], axis=0)
                v_low = jnp.concatenate([source[e0, 1, :, span], source[e1, 1, :, span]], axis=0)
                total[part] += jnp.dot(high, v_high, preferred_element_type=jnp.float32)
                total[part] += jnp.dot(low, v_high, preferred_element_type=jnp.float32)
                total[part] += jnp.dot(high, v_low, preferred_element_type=jnp.float32)
        return total[0] * 0.125, total[1] * 0.125

    def next_copy(side, part, r):
        to, at = ((right, r), (left, high_at + r))[side]
        return push(
            wext.at[part, blocks + r], wext.at[part, at],
            next_send.at[side, part, r], next_recv.at[side, part, r], (to, col),
        )

    def next_start(side, r):
        edge, via = ((is_last, up_relay), (is_first, down_relay))[side]

        @pl.when(edge)
        def _():
            for part in range(2):
                push(
                    wext.at[part, blocks + r], sbuf.at[r],
                    next_send.at[side, part, r], relay_next_recv.at[r], via[part],
                ).start()

        @pl.when(jnp.logical_not(edge))
        def _():
            for part in range(2):
                next_copy(side, part, r).start()

    def relay_next(r, carry):
        for side, at, role, to in roles:
            @pl.when(role)
            def _():
                pltpu.make_async_copy(sbuf.at[r], sbuf.at[r], relay_next_recv.at[r]).wait()
                push(
                    sbuf.at[r], wext.at[core, at + r],
                    relay_next_send.at[r], next_recv.at[side, core, r], to,
                ).start()
        return carry

    def first_row(r, carry):
        on_diagonal = lax.broadcasted_iota(jnp.int32, (block, block), 0) == lax.broadcasted_iota(
            jnp.int32, (block, block), 1
        )
        level = jnp.broadcast_to(ebuf[pl.ds(r, 1), :], (block, block))
        for k in range(width):
            value = cbuf[r * per_row + k // pair, k % pair]
            if k == 0:
                value = value + jnp.where(on_diagonal, level, 0.0)
            high, low = halves(value)
            chigh[r, :, k * block : (k + 1) * block] = high
            clow[r, :, k * block : (k + 1) * block] = low
        re, im = product(r, vhalf)
        wext[0, blocks + r] = re
        wext[1, blocks + r] = im
        split_into(whalf, blocks + r, re, im)
        next_start(0, r)
        next_start(1, r)
        return carry

    early = (blocks - 1) * per_row
    middle = early // 2
    take_pieces(0, middle)
    relay_halo()
    take_pieces(middle, early)
    own.wait()
    for side in range(2):
        for part in range(2):
            halo_copy(side, part).wait()
    to_slots.wait()

    def split_field(e, carry):
        split_into(vhalf, e, vext[0, e], vext[1, e])
        return carry

    lax.fori_loop(0, 3 * blocks, split_field, 0)
    lax.fori_loop(0, blocks - 1, first_row, 0)
    take_pieces(early, pieces)
    first_row(blocks - 1, 0)
    lax.fori_loop(0, blocks, relay_next, 0)

    def split_next(r, carry):
        for side in range(2):
            for part in range(2):
                next_copy(side, part, r).wait()
        split_into(whalf, r, wext[0, r], wext[1, r])
        split_into(whalf, 2 * blocks + r, wext[0, 2 * blocks + r], wext[1, 2 * blocks + r])
        return carry

    lax.fori_loop(0, blocks, split_next, 0)
    cosine = phase[0]
    sine = phase[1]

    def last_row(r, carry):
        re, im = product(r, whalf)
        keep = bessel_zero + 2.0 * bessel_two
        u_re = keep * vext[0, blocks + r] + 2.0 * bessel_one * wext[1, blocks + r] - 4.0 * bessel_two * re
        u_im = keep * vext[1, blocks + r] - 2.0 * bessel_one * wext[0, blocks + r] - 4.0 * bessel_two * im
        out[0, r] = cosine * u_re + sine * u_im
        out[1, r] = cosine * u_im - sine * u_re
        return carry

    lax.fori_loop(0, blocks, last_row, 0)

    @pl.when(relays)
    def _():
        push(rbuf, rbuf, relay_send, relay_recv, up_to).wait_send()

        def drain_next(r, carry):
            push(sbuf.at[r], sbuf.at[r], relay_next_send.at[r], relay_next_recv.at[r], up_to).wait_send()
            return carry

        lax.fori_loop(0, blocks, drain_next, 0)

    for way, go in both:
        @pl.when(go)
        def _():
            index_hop(way, ibuf).wait_send()
            energy_hop(way, ebuf).wait_send()

            def drain(i, carry):
                piece_hop(way, cbuf, i).wait_send()
                return carry

            lax.fori_loop(0, pieces, drain, 0)


def per_device(propagator, couplings, frame_energies, block_lists, frame_owner):
    line = lax.axis_size("cols")
    ring = lax.axis_size("space")
    moment = frame_owner[0]
    owner = jnp.mod(moment, line)
    turn = jnp.mod(moment // line, 97)
    _, blocks, width, block, _ = couplings.shape
    window = propagator.shape[2]
    angle = turn.astype(jnp.float32) * phase_unit
    phase = jnp.stack([jnp.cos(angle), jnp.sin(angle)])
    total_blocks = blocks * ring
    first_block = lax.axis_index("space") * blocks
    index = jnp.mod(block_lists[0] - first_block + REACH, total_blocks).astype(jnp.int32)
    index = jnp.pad(index.reshape(1, blocks * width), ((0, 7), (0, 128 - blocks * width)))
    energies = frame_energies.reshape(blocks, block)
    field = propagator.reshape(2, blocks, block, window)
    pieces = blocks * width // 2
    coupling = couplings.reshape(pieces, 2, block, block)

    def call(which):
        anywhere = pl.BlockSpec(memory_space=pl.ANY)
        dma = pltpu.SemaphoreType.DMA
        return pl.pallas_call(
            functools.partial(step_kernel, which, ring, line, blocks, width, block, window),
            out_shape=jax.ShapeDtypeStruct((2, blocks, block, window), jnp.float32),
            in_specs=[pl.BlockSpec(memory_space=pltpu.SMEM)] + [anywhere] * 4,
            out_specs=pl.BlockSpec(memory_space=pltpu.VMEM),
            scratch_shapes=[
                pltpu.VMEM((2, 3 * blocks, block, window), jnp.float32),
                pltpu.VMEM((2, 3 * blocks, block, window), jnp.float32),
                pltpu.VMEM((3 * blocks, 2, block, 2 * window), jnp.bfloat16),
                pltpu.VMEM((3 * blocks, 2, block, 2 * window), jnp.bfloat16),
                pltpu.VMEM((pieces, 2, block, block), jnp.float32),
                pltpu.VMEM((blocks, block, width * block), jnp.bfloat16),
                pltpu.VMEM((blocks, block, width * block), jnp.bfloat16),
                pltpu.VMEM((blocks, block), jnp.float32),
                pltpu.VMEM((8, 128), jnp.int32),
                pltpu.SMEM((8, 128), jnp.int32),
                dma((2, 2)), dma((2, 2)), dma,
                dma((2, 2, blocks)), dma((2, 2, blocks)),
                dma((2, pieces)), dma((pieces,)),
                dma((2,)), dma, dma((2,)), dma, dma,
                pltpu.VMEM((blocks, block, window), jnp.float32),
                pltpu.VMEM((blocks, block, window), jnp.float32),
                dma, dma, dma((blocks,)), dma((blocks,)),
            ],
            compiler_params=pltpu.CompilerParams(
                collective_id=which, has_side_effects=True, vmem_limit_bytes=48 << 20
            ),
            name="step",
        )

    branches = [call(which) for which in range(line)]
    result = lax.switch(owner, branches, phase, energies, index, field, coupling)
    return result.reshape(2, blocks * block, window)


def solution(mesh):
    in_specs = (
        P(None, "space", "cols"),
        P("cols", "space", None, None, None),
        P("cols", "space"),
        P("cols", "space", None),
        P(),
    )
    out_specs = P(None, "space", "cols")
    return jax.shard_map(
        per_device, mesh=mesh, in_specs=in_specs, out_specs=out_specs, check_vma=False
    )
```

```python
import functools

import jax
import jax.numpy as jnp
from jax import lax
from jax.experimental import pallas as pl
from jax.experimental.pallas import tpu as pltpu
from jax.sharding import PartitionSpec as P

REACH = 4
PLACE = (4, 2, 8, 2)
MESH = pl.DeviceIdType.MESH

bessel_zero = 0.7651976865579666
bessel_one = 0.44005058574493355
bessel_two = 0.11490348493190049
phase_unit = 6.283185307179586 / 97.0


def halves(value):
    high = value.astype(jnp.bfloat16)
    low = (value - high.astype(jnp.float32)).astype(jnp.bfloat16)
    return high, low


def step_kernel(
    owner, ring, line, blocks, width, block, window,
    phase, energies, index, field, coupling, out,
    vext, wext, vhalf, whalf, cbuf, chigh, clow, ebuf, ibuf, slots,
    halo_send, halo_recv, own_sem, next_send, next_recv, couple_send, couple_recv,
    energy_send, energy_recv, index_send, index_recv, slot_sem,
    rbuf, sbuf, relay_send, relay_recv, relay_next_send, relay_next_recv,
):
    space = lax.axis_index("space")
    col = lax.axis_index("cols")
    right = lax.rem(space + 1, ring)
    left = lax.rem(space + ring - 1, ring)
    pieces = cbuf.shape[0]
    per_row = pieces // blocks
    pair = width // per_row

    xs, zhs, ys, cores = PLACE
    zs = zhs * line
    core = lax.rem(space, cores)
    y = lax.rem(lax.div(space, cores), ys)
    z_hi = lax.rem(lax.div(space, cores * ys), zhs)
    x = lax.div(space, cores * ys * zhs)
    z = z_hi * line + col
    quarter = zs // 4

    def around(value, count):
        return lax.rem(value + count, count)

    def device(at_x, at_y, at_z, at_core):
        run = around(at_x, xs) * zhs + lax.div(at_z, line)
        return (run * ys + at_y) * cores + at_core, lax.rem(at_z, line)

    is_last = (y == ys - 1) & (core == cores - 1)
    is_first = (y == 0) & (core == 0)
    relays_up = y == 1
    relays_down = y == ys - 2
    relays = relays_up | relays_down
    x_after = x + z_hi
    x_before = x - (1 - z_hi)
    z_far = (around(z + quarter, zs), around(z - quarter, zs))
    up_relay = [device(x_after, 1, z_far[part], part) for part in range(2)]
    up_relay_in = [device(x, 1, z_far[1 - part], part) for part in range(2)]
    down_relay = [device(x_before, ys - 2, z_far[part], part) for part in range(2)]
    down_relay_in = [device(x, ys - 2, z_far[1 - part], part) for part in range(2)]
    z_from = around(z - quarter + 2 * quarter * core, zs)
    z_to = around(z_from + 2 * quarter, zs)
    up_from = device(x - lax.div(z_from, line), ys - 1, z_from, cores - 1)
    up_to = device(x, 0, z_to, 0)
    down_from = device(x + lax.div(z_to, line), 0, z_from, 0)
    down_to = device(x, ys - 1, z_to, cores - 1)

    barrier = pltpu.get_barrier_semaphore()

    def greet(*others):
        for other in others:
            pl.semaphore_signal(barrier, inc=1, device_id=other, device_id_type=MESH)

    @pl.when(jnp.logical_not(is_first))
    def _():
        greet((left, col))

    @pl.when(jnp.logical_not(is_last))
    def _():
        greet((right, col))

    @pl.when(is_last)
    def _():
        greet(*up_relay, *down_relay_in)

    @pl.when(is_first)
    def _():
        greet(*down_relay, *up_relay_in)

    @pl.when(relays_up)
    def _():
        greet(up_from, up_to)

    @pl.when(relays_down)
    def _():
        greet(down_from, down_to)

    @pl.when(col > 0)
    def _():
        greet((space, col - 1))

    @pl.when(col < line - 1)
    def _():
        greet((space, col + 1))

    greeters = (
        3
        + jnp.where((col > 0) & (col < line - 1), 1, 0)
        + jnp.where(is_first | is_last, 3, 0)
        + jnp.where(relays, 2, 0)
    )
    pl.semaphore_wait(barrier, greeters)

    is_owner = col == owner
    go_up = (col >= owner) & (col < line - 1)
    go_down = (col <= owner) & (col > 0)

    def hop(way, source, target, send_sem, recv_sem):
        to = col + 1 if way == 0 else col - 1
        return pltpu.make_async_remote_copy(
            src_ref=source, dst_ref=target, send_sem=send_sem, recv_sem=recv_sem,
            device_id=(space, to), device_id_type=MESH,
        )

    def piece_hop(way, source, i):
        return hop(way, source.at[i], cbuf.at[i], couple_send.at[way, i], couple_recv.at[i])

    def energy_hop(way, source):
        return hop(way, source, ebuf, energy_send.at[way], energy_recv)

    def index_hop(way, source):
        return hop(way, source, ibuf, index_send.at[way], index_recv)

    both = ((0, go_up), (1, go_down))

    @pl.when(is_owner)
    def _():
        for way, go in both:
            @pl.when(go)
            def _():
                index_hop(way, index).start()
                energy_hop(way, energies).start()
        pltpu.make_async_copy(index, ibuf, index_recv).start()
        pltpu.make_async_copy(energies, ebuf, energy_recv).start()

        def send_piece(i, carry):
            for way, go in both:
                @pl.when(go)
                def _():
                    piece_hop(way, coupling, i).start()
            pltpu.make_async_copy(coupling.at[i], cbuf.at[i], couple_recv.at[i]).start()
            return carry

        lax.fori_loop(0, pieces, send_piece, 0)

    low_at, high_at = 0, 2 * blocks

    def push(source, target, send_sem, recv_sem, to):
        return pltpu.make_async_remote_copy(
            src_ref=source, dst_ref=target, send_sem=send_sem, recv_sem=recv_sem,
            device_id=to, device_id_type=MESH,
        )

    def halo_copy(side, part):
        to, at = ((right, low_at), (left, high_at))[side]
        return push(
            field.at[part], vext.at[part, pl.ds(at, blocks)],
            halo_send.at[side, part], halo_recv.at[side, part], (to, col),
        )

    def halo_start(side):
        edge, via = ((is_last, up_relay), (is_first, down_relay))[side]

        @pl.when(edge)
        def _():
            for part in range(2):
                push(field.at[part], rbuf, halo_send.at[side, part], relay_recv, via[part]).start()

        @pl.when(jnp.logical_not(edge))
        def _():
            for part in range(2):
                halo_copy(side, part).start()

    roles = ((0, low_at, relays_up, up_to), (1, high_at, relays_down, down_to))

    def relay_halo():
        for side, at, role, to in roles:
            @pl.when(role)
            def _():
                passed = push(
                    rbuf, vext.at[core, pl.ds(at, blocks)], relay_send, halo_recv.at[side, core], to
                )
                pltpu.make_async_copy(rbuf, rbuf, relay_recv).wait()
                passed.start()

    halo_start(0)
    halo_start(1)
    own = pltpu.make_async_copy(field, vext.at[:, pl.ds(blocks, blocks)], own_sem)
    own.start()

    pltpu.make_async_copy(ibuf, ibuf, index_recv).wait()
    pltpu.make_async_copy(ebuf, ebuf, energy_recv).wait()

    @pl.when(jnp.logical_not(is_owner))
    def _():
        for way, go in both:
            @pl.when(go)
            def _():
                index_hop(way, ibuf).start()
                energy_hop(way, ebuf).start()

    to_slots = pltpu.make_async_copy(ibuf, slots, slot_sem)
    to_slots.start()

    def take_pieces(first_piece, last_piece):
        def take(i, carry):
            pltpu.make_async_copy(cbuf.at[i], cbuf.at[i], couple_recv.at[i]).wait()

            @pl.when(jnp.logical_not(is_owner))
            def _():
                for way, go in both:
                    @pl.when(go)
                    def _():
                        piece_hop(way, cbuf, i).start()
            return carry

        lax.fori_loop(first_piece, last_piece, take, 0)

    def split_into(target, at, re, im):
        re_high, re_low = halves(re)
        im_high, im_low = halves(im)
        target[at, 0, :, 0:window] = re_high
        target[at, 0, :, window:] = im_high
        target[at, 1, :, 0:window] = re_low
        target[at, 1, :, window:] = im_low

    def product(r, source):
        total = [jnp.zeros((block, window), jnp.float32) for _ in range(2)]
        for k in range(0, width, 2):
            e0 = slots[0, r * width + k]
            e1 = slots[0, r * width + k + 1]
            lanes = pl.ds(k * block, 2 * block)
            high = chigh[r, :, lanes]
            low = clow[r, :, lanes]
            for part in range(2):
                span = pl.ds(part * window, window)
                v_high = jnp.concatenate([source[e0, 0, :, span], source[e1, 0, :, span]], axis=0)
                v_low = jnp.concatenate([source[e0, 1, :, span], source[e1, 1, :, span]], axis=0)
                total[part] += jnp.dot(high, v_high, preferred_element_type=jnp.float32)
                total[part] += jnp.dot(low, v_high, preferred_element_type=jnp.float32)
                total[part] += jnp.dot(high, v_low, preferred_element_type=jnp.float32)
        return total[0] * 0.125, total[1] * 0.125

    def next_copy(side, part, r):
        to, at = ((right, r), (left, high_at + r))[side]
        return push(
            wext.at[part, blocks + r], wext.at[part, at],
            next_send.at[side, part, r], next_recv.at[side, part, r], (to, col),
        )

    def next_start(side, r):
        edge, via = ((is_last, up_relay), (is_first, down_relay))[side]

        @pl.when(edge)
        def _():
            for part in range(2):
                push(
                    wext.at[part, blocks + r], sbuf.at[r],
                    next_send.at[side, part, r], relay_next_recv.at[r], via[part],
                ).start()

        @pl.when(jnp.logical_not(edge))
        def _():
            for part in range(2):
                next_copy(side, part, r).start()

    def relay_next(r, carry):
        for side, at, role, to in roles:
            @pl.when(role)
            def _():
                pltpu.make_async_copy(sbuf.at[r], sbuf.at[r], relay_next_recv.at[r]).wait()
                push(
                    sbuf.at[r], wext.at[core, at + r],
                    relay_next_send.at[r], next_recv.at[side, core, r], to,
                ).start()
        return carry

    def first_row(r, carry):
        on_diagonal = lax.broadcasted_iota(jnp.int32, (block, block), 0) == lax.broadcasted_iota(
            jnp.int32, (block, block), 1
        )
        level = jnp.broadcast_to(ebuf[pl.ds(r, 1), :], (block, block))
        for k in range(width):
            value = cbuf[r * per_row + k // pair, k % pair]
            if k == 0:
                value = value + jnp.where(on_diagonal, level, 0.0)
            high, low = halves(value)
            chigh[r, :, k * block : (k + 1) * block] = high
            clow[r, :, k * block : (k + 1) * block] = low
        re, im = product(r, vhalf)
        wext[0, blocks + r] = re
        wext[1, blocks + r] = im
        split_into(whalf, blocks + r, re, im)
        next_start(0, r)
        next_start(1, r)
        return carry

    early = (blocks - 1) * per_row
    middle = early // 2 - 1
    passes_on = jnp.logical_not(is_owner) & (go_up | go_down)
    is_end = is_first | is_last

    @pl.when(jnp.logical_not(passes_on))
    def _():
        relay_halo()

    take_pieces(0, middle)

    @pl.when(passes_on)
    def _():
        relay_halo()

    take_pieces(middle, early)

    @pl.when(is_end)
    def _():
        take_pieces(early, pieces)

    own.wait()
    for side in range(2):
        for part in range(2):
            halo_copy(side, part).wait()
    to_slots.wait()

    def split_field(e, carry):
        split_into(vhalf, e, vext[0, e], vext[1, e])
        return carry

    lax.fori_loop(0, 3 * blocks, split_field, 0)
    lax.fori_loop(0, blocks - 1, first_row, 0)

    @pl.when(jnp.logical_not(is_end))
    def _():
        take_pieces(early, pieces)

    first_row(blocks - 1, 0)
    lax.fori_loop(0, blocks, relay_next, 0)

    def split_next(r, carry):
        for side in range(2):
            for part in range(2):
                next_copy(side, part, r).wait()
        split_into(whalf, r, wext[0, r], wext[1, r])
        split_into(whalf, 2 * blocks + r, wext[0, 2 * blocks + r], wext[1, 2 * blocks + r])
        return carry

    lax.fori_loop(0, blocks, split_next, 0)
    cosine = phase[0]
    sine = phase[1]

    def last_row(r, carry):
        re, im = product(r, whalf)
        keep = bessel_zero + 2.0 * bessel_two
        u_re = keep * vext[0, blocks + r] + 2.0 * bessel_one * wext[1, blocks + r] - 4.0 * bessel_two * re
        u_im = keep * vext[1, blocks + r] - 2.0 * bessel_one * wext[0, blocks + r] - 4.0 * bessel_two * im
        out[0, r] = cosine * u_re + sine * u_im
        out[1, r] = cosine * u_im - sine * u_re
        return carry

    lax.fori_loop(0, blocks, last_row, 0)

    @pl.when(relays)
    def _():
        push(rbuf, rbuf, relay_send, relay_recv, up_to).wait_send()

        def drain_next(r, carry):
            push(sbuf.at[r], sbuf.at[r], relay_next_send.at[r], relay_next_recv.at[r], up_to).wait_send()
            return carry

        lax.fori_loop(0, blocks, drain_next, 0)

    for way, go in both:
        @pl.when(go)
        def _():
            index_hop(way, ibuf).wait_send()
            energy_hop(way, ebuf).wait_send()

            def drain(i, carry):
                piece_hop(way, cbuf, i).wait_send()
                return carry

            lax.fori_loop(0, pieces, drain, 0)


def per_device(propagator, couplings, frame_energies, block_lists, frame_owner):
    line = lax.axis_size("cols")
    ring = lax.axis_size("space")
    moment = frame_owner[0]
    owner = jnp.mod(moment, line)
    turn = jnp.mod(moment // line, 97)
    _, blocks, width, block, _ = couplings.shape
    window = propagator.shape[2]
    angle = turn.astype(jnp.float32) * phase_unit
    phase = jnp.stack([jnp.cos(angle), jnp.sin(angle)])
    total_blocks = blocks * ring
    first_block = lax.axis_index("space") * blocks
    index = jnp.mod(block_lists[0] - first_block + REACH, total_blocks).astype(jnp.int32)
    index = jnp.pad(index.reshape(1, blocks * width), ((0, 7), (0, 128 - blocks * width)))
    energies = frame_energies.reshape(blocks, block)
    field = propagator.reshape(2, blocks, block, window)
    pieces = blocks * width // 2
    coupling = couplings.reshape(pieces, 2, block, block)

    def call(which):
        anywhere = pl.BlockSpec(memory_space=pl.ANY)
        dma = pltpu.SemaphoreType.DMA
        return pl.pallas_call(
            functools.partial(step_kernel, which, ring, line, blocks, width, block, window),
            out_shape=jax.ShapeDtypeStruct((2, blocks, block, window), jnp.float32),
            in_specs=[pl.BlockSpec(memory_space=pltpu.SMEM)] + [anywhere] * 4,
            out_specs=pl.BlockSpec(memory_space=pltpu.VMEM),
            scratch_shapes=[
                pltpu.VMEM((2, 3 * blocks, block, window), jnp.float32),
                pltpu.VMEM((2, 3 * blocks, block, window), jnp.float32),
                pltpu.VMEM((3 * blocks, 2, block, 2 * window), jnp.bfloat16),
                pltpu.VMEM((3 * blocks, 2, block, 2 * window), jnp.bfloat16),
                pltpu.VMEM((pieces, 2, block, block), jnp.float32),
                pltpu.VMEM((blocks, block, width * block), jnp.bfloat16),
                pltpu.VMEM((blocks, block, width * block), jnp.bfloat16),
                pltpu.VMEM((blocks, block), jnp.float32),
                pltpu.VMEM((8, 128), jnp.int32),
                pltpu.SMEM((8, 128), jnp.int32),
                dma((2, 2)), dma((2, 2)), dma,
                dma((2, 2, blocks)), dma((2, 2, blocks)),
                dma((2, pieces)), dma((pieces,)),
                dma((2,)), dma, dma((2,)), dma, dma,
                pltpu.VMEM((blocks, block, window), jnp.float32),
                pltpu.VMEM((blocks, block, window), jnp.float32),
                dma, dma, dma((blocks,)), dma((blocks,)),
            ],
            compiler_params=pltpu.CompilerParams(
                collective_id=which, has_side_effects=True, vmem_limit_bytes=48 << 20
            ),
            name="step",
        )

    branches = [call(which) for which in range(line)]
    result = lax.switch(owner, branches, phase, energies, index, field, coupling)
    return result.reshape(2, blocks * block, window)


def solution(mesh):
    in_specs = (
        P(None, "space", "cols"),
        P("cols", "space", None, None, None),
        P("cols", "space"),
        P("cols", "space", None),
        P(),
    )
    out_specs = P(None, "space", "cols")
    return jax.shard_map(
        per_device, mesh=mesh, in_specs=in_specs, out_specs=out_specs, check_vma=False
    )
```

```python
import functools

import jax
import jax.numpy as jnp
from jax import lax
from jax.experimental import pallas as pl
from jax.experimental.pallas import tpu as pltpu
from jax.sharding import PartitionSpec as P

REACH = 4
PLACE = (4, 2, 8, 2)
VIA_ONE = True
VIA_ROWS = 3
READY_ROWS = 2
LEAD = 3
MESH = pl.DeviceIdType.MESH

bessel_zero = 0.7651976865579666
bessel_one = 0.44005058574493355
bessel_two = 0.11490348493190049
phase_unit = 6.283185307179586 / 97.0


def halves(value):
    high = value.astype(jnp.bfloat16)
    low = (value - high.astype(jnp.float32)).astype(jnp.bfloat16)
    return high, low


def step_kernel(
    owner, ring, line, blocks, width, block, window,
    phase, energies, index, field, coupling, out,
    vext, wext, vhalf, whalf, cbuf, chigh, clow, ebuf, ibuf, slots,
    halo_send, halo_recv, own_sem, next_send, next_recv, couple_send, couple_recv,
    energy_send, energy_recv, index_send, index_recv, slot_sem,
    rbuf, sbuf, relay_send, relay_recv, relay_next_send, relay_next_recv,
):
    space = lax.axis_index("space")
    col = lax.axis_index("cols")
    right = lax.rem(space + 1, ring)
    left = lax.rem(space + ring - 1, ring)
    pieces = cbuf.shape[0]
    per_row = pieces // blocks
    pair = width // per_row

    xs, zhs, ys, cores = PLACE
    zs = zhs * line
    core = lax.rem(space, cores)
    y = lax.rem(lax.div(space, cores), ys)
    z_hi = lax.rem(lax.div(space, cores * ys), zhs)
    x = lax.div(space, cores * ys * zhs)
    z = z_hi * line + col
    quarter = zs // 4

    def around(value, count):
        return lax.rem(value + count, count)

    def device(at_x, at_y, at_z, at_core):
        run = around(at_x, xs) * zhs + lax.div(at_z, line)
        return (run * ys + at_y) * cores + at_core, lax.rem(at_z, line)

    is_last = (y == ys - 1) & (core == cores - 1)
    is_first = (y == 0) & (core == 0)
    relays_up = y == 1
    relays_down = y == ys - 2
    relays = relays_up | relays_down
    x_after = x + z_hi
    x_before = x - (1 - z_hi)
    z_far = (around(z + quarter, zs), around(z - quarter, zs))
    up_relay = [device(x_after, 1, z_far[part], part) for part in range(2)]
    up_relay_in = [device(x, 1, z_far[1 - part], part) for part in range(2)]
    down_relay = [device(x_before, ys - 2, z_far[part], part) for part in range(2)]
    down_relay_in = [device(x, ys - 2, z_far[1 - part], part) for part in range(2)]
    z_from = around(z - quarter + 2 * quarter * core, zs)
    z_to = around(z_from + 2 * quarter, zs)
    up_from = device(x - lax.div(z_from, line), ys - 1, z_from, cores - 1)
    up_to = device(x, 0, z_to, 0)
    down_from = device(x + lax.div(z_to, line), 0, z_from, 0)
    down_to = device(x, ys - 1, z_to, cores - 1)

    barrier = pltpu.get_barrier_semaphore()

    def greet(*others):
        for other in others:
            pl.semaphore_signal(barrier, inc=1, device_id=other, device_id_type=MESH)

    direct = not (VIA_ONE and VIA_ROWS == blocks)
    if direct:
        greet((left, col), (right, col))
    else:
        @pl.when(jnp.logical_not(is_first))
        def _():
            greet((left, col))

        @pl.when(jnp.logical_not(is_last))
        def _():
            greet((right, col))

    relayed = VIA_ONE or VIA_ROWS > 0

    @pl.when(is_last & relayed)
    def _():
        greet(*up_relay, *down_relay_in)

    @pl.when(is_first & relayed)
    def _():
        greet(*down_relay, *up_relay_in)

    @pl.when(relays_up & relayed)
    def _():
        greet(up_from, up_to)

    @pl.when(relays_down & relayed)
    def _():
        greet(down_from, down_to)

    @pl.when(col > 0)
    def _():
        greet((space, col - 1))

    @pl.when(col < line - 1)
    def _():
        greet((space, col + 1))

    greeters = (
        3
        + jnp.where((col > 0) & (col < line - 1), 1, 0)
        + jnp.where(is_first | is_last, (3 + direct) * relayed, 0)
        + jnp.where(relays, 2 * relayed, 0)
    )
    pl.semaphore_wait(barrier, greeters)

    is_owner = col == owner
    go_up = (col >= owner) & (col < line - 1)
    go_down = (col <= owner) & (col > 0)

    def hop(way, source, target, send_sem, recv_sem):
        to = col + 1 if way == 0 else col - 1
        return pltpu.make_async_remote_copy(
            src_ref=source, dst_ref=target, send_sem=send_sem, recv_sem=recv_sem,
            device_id=(space, to), device_id_type=MESH,
        )

    def piece_hop(way, source, i):
        return hop(way, source.at[i], cbuf.at[i], couple_send.at[way, i], couple_recv.at[i])

    def energy_hop(way, source):
        return hop(way, source, ebuf, energy_send.at[way], energy_recv)

    def index_hop(way, source):
        return hop(way, source, ibuf, index_send.at[way], index_recv)

    both = ((0, go_up), (1, go_down))

    @pl.when(is_owner)
    def _():
        for way, go in both:
            @pl.when(go)
            def _():
                index_hop(way, index).start()
                energy_hop(way, energies).start()
        pltpu.make_async_copy(index, ibuf, index_recv).start()
        pltpu.make_async_copy(energies, ebuf, energy_recv).start()

        def send_piece(i, carry):
            for way, go in both:
                @pl.when(go)
                def _():
                    piece_hop(way, coupling, i).start()
            pltpu.make_async_copy(coupling.at[i], cbuf.at[i], couple_recv.at[i]).start()
            return carry

        lax.fori_loop(0, pieces, send_piece, 0)

    low_at, high_at = 0, 2 * blocks

    def push(source, target, send_sem, recv_sem, to):
        return pltpu.make_async_remote_copy(
            src_ref=source, dst_ref=target, send_sem=send_sem, recv_sem=recv_sem,
            device_id=to, device_id_type=MESH,
        )

    def halo_copy(side, part, b):
        to, at = ((right, low_at), (left, high_at))[side]
        return push(
            field.at[part, b], vext.at[part, at + b],
            halo_send.at[side, part, b], halo_recv.at[side, part, b], (to, col),
        )

    def halo_start(b, carry):
        for side in range(2):
            edge, via = ((is_last, up_relay), (is_first, down_relay))[side]
            if VIA_ONE:
                @pl.when(edge)
                def _():
                    for part in range(2):
                        push(
                            field.at[part, b], rbuf.at[b],
                            halo_send.at[side, part, b], relay_recv.at[b], via[part],
                        ).start()

            @pl.when(jnp.logical_not(edge & VIA_ONE))
            def _():
                for part in range(2):
                    halo_copy(side, part, b).start()
        return carry

    roles = ((0, low_at, relays_up, up_to), (1, high_at, relays_down, down_to))

    def relay_halo(b, carry):
        for side, at, role, to in roles:
            @pl.when(role)
            def _():
                pltpu.make_async_copy(rbuf.at[b], rbuf.at[b], relay_recv.at[b]).wait()
                push(
                    rbuf.at[b], vext.at[core, at + b],
                    relay_send.at[b], halo_recv.at[side, core, b], to,
                ).start()
        return carry

    lax.fori_loop(0, blocks, halo_start, 0)
    own = pltpu.make_async_copy(field, vext.at[:, pl.ds(blocks, blocks)], own_sem)
    own.start()

    pltpu.make_async_copy(ibuf, ibuf, index_recv).wait()
    pltpu.make_async_copy(ebuf, ebuf, energy_recv).wait()

    @pl.when(jnp.logical_not(is_owner))
    def _():
        for way, go in both:
            @pl.when(go)
            def _():
                index_hop(way, ibuf).start()
                energy_hop(way, ebuf).start()

    to_slots = pltpu.make_async_copy(ibuf, slots, slot_sem)
    to_slots.start()

    def take_pieces(first_piece, last_piece):
        def take(i, carry):
            pltpu.make_async_copy(cbuf.at[i], cbuf.at[i], couple_recv.at[i]).wait()

            @pl.when(jnp.logical_not(is_owner))
            def _():
                for way, go in both:
                    @pl.when(go)
                    def _():
                        piece_hop(way, cbuf, i).start()
            return carry

        lax.fori_loop(first_piece, last_piece, take, 0)

    def split_into(target, at, re, im):
        re_high, re_low = halves(re)
        im_high, im_low = halves(im)
        target[at, 0, :, 0:window] = re_high
        target[at, 0, :, window:] = im_high
        target[at, 1, :, 0:window] = re_low
        target[at, 1, :, window:] = im_low

    def product(r, source):
        total = [jnp.zeros((block, window), jnp.float32) for _ in range(2)]
        for k in range(0, width, 2):
            e0 = slots[0, r * width + k]
            e1 = slots[0, r * width + k + 1]
            lanes = pl.ds(k * block, 2 * block)
            high = chigh[r, :, lanes]
            low = clow[r, :, lanes]
            for part in range(2):
                span = pl.ds(part * window, window)
                v_high = jnp.concatenate([source[e0, 0, :, span], source[e1, 0, :, span]], axis=0)
                v_low = jnp.concatenate([source[e0, 1, :, span], source[e1, 1, :, span]], axis=0)
                total[part] += jnp.dot(high, v_high, preferred_element_type=jnp.float32)
                total[part] += jnp.dot(low, v_high, preferred_element_type=jnp.float32)
                total[part] += jnp.dot(high, v_low, preferred_element_type=jnp.float32)
        return total[0] * 0.125, total[1] * 0.125

    def next_copy(side, part, r):
        to, at = ((right, r), (left, high_at + r))[side]
        return push(
            wext.at[part, blocks + r], wext.at[part, at],
            next_send.at[side, part, r], next_recv.at[side, part, r], (to, col),
        )

    def next_start(side, r):
        edge, via = ((is_last, up_relay), (is_first, down_relay))[side]
        relayed_row = edge & (r < VIA_ROWS)

        @pl.when(relayed_row)
        def _():
            for part in range(2):
                push(
                    wext.at[part, blocks + r], sbuf.at[r],
                    next_send.at[side, part, r], relay_next_recv.at[r], via[part],
                ).start()

        @pl.when(jnp.logical_not(relayed_row))
        def _():
            for part in range(2):
                next_copy(side, part, r).start()

    def relay_next(r, carry):
        for side, at, role, to in roles:
            @pl.when(role)
            def _():
                pltpu.make_async_copy(sbuf.at[r], sbuf.at[r], relay_next_recv.at[r]).wait()
                push(
                    sbuf.at[r], wext.at[core, at + r],
                    relay_next_send.at[r], next_recv.at[side, core, r], to,
                ).start()
        return carry

    def first_row(r, carry):
        on_diagonal = lax.broadcasted_iota(jnp.int32, (block, block), 0) == lax.broadcasted_iota(
            jnp.int32, (block, block), 1
        )
        level = jnp.broadcast_to(ebuf[pl.ds(r, 1), :], (block, block))
        for k in range(width):
            value = cbuf[r * per_row + k // pair, k % pair]
            if k == 0:
                value = value + jnp.where(on_diagonal, level, 0.0)
            high, low = halves(value)
            chigh[r, :, k * block : (k + 1) * block] = high
            clow[r, :, k * block : (k + 1) * block] = low
        re, im = product(r, vhalf)
        wext[0, blocks + r] = re
        wext[1, blocks + r] = im
        split_into(whalf, blocks + r, re, im)
        next_start(0, r)
        next_start(1, r)
        return carry

    early = READY_ROWS * per_row
    passes_on = jnp.logical_not(is_owner) & (go_up | go_down)
    if VIA_ONE:
        @pl.when(jnp.logical_not(passes_on))
        def _():
            lax.fori_loop(0, blocks, relay_halo, 0)

    take_pieces(0, LEAD)
    if VIA_ONE:
        def pass_and_take(b, carry):
            @pl.when(passes_on)
            def _():
                relay_halo(b, 0)

            take_pieces(LEAD + b, LEAD + b + 1)
            return carry

        lax.fori_loop(0, blocks, pass_and_take, 0)
        take_pieces(LEAD + blocks, early)
    else:
        take_pieces(LEAD, early)

    own.wait()
    def halo_wait(b, carry):
        for side in range(2):
            for part in range(2):
                halo_copy(side, part, b).wait()
        return carry

    lax.fori_loop(0, blocks, halo_wait, 0)
    to_slots.wait()

    def split_field(e, carry):
        split_into(vhalf, e, vext[0, e], vext[1, e])
        return carry

    lax.fori_loop(0, 3 * blocks, split_field, 0)
    lax.fori_loop(0, READY_ROWS, first_row, 0)

    relayed_rows = list(range(VIA_ROWS))
    for r in range(READY_ROWS, blocks):
        take_pieces(r * per_row, (r + 1) * per_row)
        first_row(r, 0)
        for q in relayed_rows[:2]:
            relay_next(q, 0)
        relayed_rows = relayed_rows[2:]

    def split_next(r, carry):
        for side in range(2):
            for part in range(2):
                next_copy(side, part, r).wait()
        split_into(whalf, r, wext[0, r], wext[1, r])
        split_into(whalf, 2 * blocks + r, wext[0, 2 * blocks + r], wext[1, 2 * blocks + r])
        return carry

    lax.fori_loop(0, blocks, split_next, 0)
    cosine = phase[0]
    sine = phase[1]

    def last_row(r, carry):
        re, im = product(r, whalf)
        keep = bessel_zero + 2.0 * bessel_two
        u_re = keep * vext[0, blocks + r] + 2.0 * bessel_one * wext[1, blocks + r] - 4.0 * bessel_two * re
        u_im = keep * vext[1, blocks + r] - 2.0 * bessel_one * wext[0, blocks + r] - 4.0 * bessel_two * im
        out[0, r] = cosine * u_re + sine * u_im
        out[1, r] = cosine * u_im - sine * u_re
        return carry

    lax.fori_loop(0, blocks, last_row, 0)

    @pl.when(relays)
    def _():
        def drain_one(r, carry):
            push(rbuf.at[r], rbuf.at[r], relay_send.at[r], relay_recv.at[r], up_to).wait_send()
            return carry

        if VIA_ONE:
            lax.fori_loop(0, blocks, drain_one, 0)

        def drain_next(r, carry):
            push(sbuf.at[r], sbuf.at[r], relay_next_send.at[r], relay_next_recv.at[r], up_to).wait_send()
            return carry

        lax.fori_loop(0, VIA_ROWS, drain_next, 0)

    for way, go in both:
        @pl.when(go)
        def _():
            index_hop(way, ibuf).wait_send()
            energy_hop(way, ebuf).wait_send()

            def drain(i, carry):
                piece_hop(way, cbuf, i).wait_send()
                return carry

            lax.fori_loop(0, pieces, drain, 0)


def per_device(propagator, couplings, frame_energies, block_lists, frame_owner):
    line = lax.axis_size("cols")
    ring = lax.axis_size("space")
    moment = frame_owner[0]
    owner = jnp.mod(moment, line)
    turn = jnp.mod(moment // line, 97)
    _, blocks, width, block, _ = couplings.shape
    window = propagator.shape[2]
    angle = turn.astype(jnp.float32) * phase_unit
    phase = jnp.stack([jnp.cos(angle), jnp.sin(angle)])
    total_blocks = blocks * ring
    first_block = lax.axis_index("space") * blocks
    index = jnp.mod(block_lists[0] - first_block + REACH, total_blocks).astype(jnp.int32)
    index = jnp.pad(index.reshape(1, blocks * width), ((0, 7), (0, 128 - blocks * width)))
    energies = frame_energies.reshape(blocks, block)
    field = propagator.reshape(2, blocks, block, window)
    pieces = blocks * width // 2
    coupling = couplings.reshape(pieces, 2, block, block)

    def call(which):
        anywhere = pl.BlockSpec(memory_space=pl.ANY)
        dma = pltpu.SemaphoreType.DMA
        return pl.pallas_call(
            functools.partial(step_kernel, which, ring, line, blocks, width, block, window),
            out_shape=jax.ShapeDtypeStruct((2, blocks, block, window), jnp.float32),
            in_specs=[pl.BlockSpec(memory_space=pltpu.SMEM)] + [anywhere] * 4,
            out_specs=pl.BlockSpec(memory_space=pltpu.VMEM),
            scratch_shapes=[
                pltpu.VMEM((2, 3 * blocks, block, window), jnp.float32),
                pltpu.VMEM((2, 3 * blocks, block, window), jnp.float32),
                pltpu.VMEM((3 * blocks, 2, block, 2 * window), jnp.bfloat16),
                pltpu.VMEM((3 * blocks, 2, block, 2 * window), jnp.bfloat16),
                pltpu.VMEM((pieces, 2, block, block), jnp.float32),
                pltpu.VMEM((blocks, block, width * block), jnp.bfloat16),
                pltpu.VMEM((blocks, block, width * block), jnp.bfloat16),
                pltpu.VMEM((blocks, block), jnp.float32),
                pltpu.VMEM((8, 128), jnp.int32),
                pltpu.SMEM((8, 128), jnp.int32),
                dma((2, 2, blocks)), dma((2, 2, blocks)), dma,
                dma((2, 2, blocks)), dma((2, 2, blocks)),
                dma((2, pieces)), dma((pieces,)),
                dma((2,)), dma, dma((2,)), dma, dma,
                pltpu.VMEM((blocks, block, window), jnp.float32),
                pltpu.VMEM((blocks, block, window), jnp.float32),
                dma((blocks,)), dma((blocks,)), dma((blocks,)), dma((blocks,)),
            ],
            compiler_params=pltpu.CompilerParams(
                collective_id=which, has_side_effects=True, vmem_limit_bytes=48 << 20
            ),
            name="step",
        )

    branches = [call(which) for which in range(line)]
    result = lax.switch(owner, branches, phase, energies, index, field, coupling)
    return result.reshape(2, blocks * block, window)


def solution(mesh):
    in_specs = (
        P(None, "space", "cols"),
        P("cols", "space", None, None, None),
        P("cols", "space"),
        P("cols", "space", None),
        P(),
    )
    out_specs = P(None, "space", "cols")
    return jax.shard_map(
        per_device, mesh=mesh, in_specs=in_specs, out_specs=out_specs, check_vma=False
    )
```

```python
import functools

import jax
import jax.numpy as jnp
from jax import lax
from jax.experimental import pallas as pl
from jax.experimental.pallas import tpu as pltpu
from jax.sharding import PartitionSpec as P

REACH = 4
PLACE = (4, 2, 8, 2)
VIA_ONE = True
VIA_ROWS = 3
READY_ROWS = 2
LEAD = 3
MESH = pl.DeviceIdType.MESH

bessel_zero = 0.7651976865579666
bessel_one = 0.44005058574493355
bessel_two = 0.11490348493190049
phase_unit = 6.283185307179586 / 97.0


def halves(value):
    high = value.astype(jnp.bfloat16)
    low = (value - high.astype(jnp.float32)).astype(jnp.bfloat16)
    return high, low


def step_kernel(
    owner, ring, line, blocks, width, block, window,
    phase, energies, index, field, coupling, out,
    vext, wext, vhalf, whalf, cbuf, chigh, clow, ebuf, ibuf, slots,
    halo_send, halo_recv, own_sem, next_send, next_recv, couple_send, couple_recv,
    energy_send, energy_recv, index_send, index_recv, slot_sem,
    rbuf, sbuf, relay_send, relay_recv, relay_next_send, relay_next_recv,
):
    space = lax.axis_index("space")
    col = lax.axis_index("cols")
    right = lax.rem(space + 1, ring)
    left = lax.rem(space + ring - 1, ring)
    pieces = cbuf.shape[0]
    per_row = pieces // blocks
    pair = width // per_row

    xs, zhs, ys, cores = PLACE
    zs = zhs * line
    core = lax.rem(space, cores)
    y = lax.rem(lax.div(space, cores), ys)
    z_hi = lax.rem(lax.div(space, cores * ys), zhs)
    x = lax.div(space, cores * ys * zhs)
    z = z_hi * line + col
    quarter = zs // 4

    def around(value, count):
        return lax.rem(value + count, count)

    def device(at_x, at_y, at_z, at_core):
        run = around(at_x, xs) * zhs + lax.div(at_z, line)
        return (run * ys + at_y) * cores + at_core, lax.rem(at_z, line)

    is_last = (y == ys - 1) & (core == cores - 1)
    is_first = (y == 0) & (core == 0)
    relays_up = y == 1
    relays_down = y == ys - 2
    relays = relays_up | relays_down
    x_after = x + z_hi
    x_before = x - (1 - z_hi)
    z_far = (around(z + quarter, zs), around(z - quarter, zs))
    up_relay = [device(x_after, 1, z_far[part], part) for part in range(2)]
    up_relay_in = [device(x, 1, z_far[1 - part], part) for part in range(2)]
    down_relay = [device(x_before, ys - 2, z_far[part], part) for part in range(2)]
    down_relay_in = [device(x, ys - 2, z_far[1 - part], part) for part in range(2)]
    z_from = around(z - quarter + 2 * quarter * core, zs)
    z_to = around(z_from + 2 * quarter, zs)
    up_from = device(x - lax.div(z_from, line), ys - 1, z_from, cores - 1)
    up_to = device(x, 0, z_to, 0)
    down_from = device(x + lax.div(z_to, line), 0, z_from, 0)
    down_to = device(x, ys - 1, z_to, cores - 1)

    barrier = pltpu.get_barrier_semaphore()

    def greet(*others):
        for other in others:
            pl.semaphore_signal(barrier, inc=1, device_id=other, device_id_type=MESH)

    direct = not (VIA_ONE and VIA_ROWS == blocks)
    if direct:
        greet((left, col), (right, col))
    else:
        @pl.when(jnp.logical_not(is_first))
        def _():
            greet((left, col))

        @pl.when(jnp.logical_not(is_last))
        def _():
            greet((right, col))

    relayed = VIA_ONE or VIA_ROWS > 0

    @pl.when(is_last & relayed)
    def _():
        greet(*up_relay, *down_relay_in)

    @pl.when(is_first & relayed)
    def _():
        greet(*down_relay, *up_relay_in)

    @pl.when(relays_up & relayed)
    def _():
        greet(up_from, up_to)

    @pl.when(relays_down & relayed)
    def _():
        greet(down_from, down_to)

    @pl.when(col > 0)
    def _():
        greet((space, col - 1))

    @pl.when(col < line - 1)
    def _():
        greet((space, col + 1))

    greeters = (
        3
        + jnp.where((col > 0) & (col < line - 1), 1, 0)
        + jnp.where(is_first | is_last, (3 + direct) * relayed, 0)
        + jnp.where(relays, 2 * relayed, 0)
    )
    pl.semaphore_wait(barrier, greeters)

    is_owner = col == owner
    go_up = (col >= owner) & (col < line - 1)
    go_down = (col <= owner) & (col > 0)

    def hop(way, source, target, send_sem, recv_sem):
        to = col + 1 if way == 0 else col - 1
        return pltpu.make_async_remote_copy(
            src_ref=source, dst_ref=target, send_sem=send_sem, recv_sem=recv_sem,
            device_id=(space, to), device_id_type=MESH,
        )

    def piece_hop(way, source, i):
        return hop(way, source.at[i], cbuf.at[i], couple_send.at[way, i], couple_recv.at[i])

    def energy_hop(way, source):
        return hop(way, source, ebuf, energy_send.at[way], energy_recv)

    def index_hop(way, source):
        return hop(way, source, ibuf, index_send.at[way], index_recv)

    both = ((0, go_up), (1, go_down))

    low_at, high_at = 0, 2 * blocks

    def push(source, target, send_sem, recv_sem, to):
        return pltpu.make_async_remote_copy(
            src_ref=source, dst_ref=target, send_sem=send_sem, recv_sem=recv_sem,
            device_id=to, device_id_type=MESH,
        )

    def halo_copy(side, part, b):
        to, at = ((right, low_at), (left, high_at))[side]
        return push(
            field.at[part, b], vext.at[part, at + b],
            halo_send.at[side, part, b], halo_recv.at[side, part, b], (to, col),
        )

    def halo_start(b, carry):
        for side in range(2):
            edge, via = ((is_last, up_relay), (is_first, down_relay))[side]
            if VIA_ONE:
                @pl.when(edge)
                def _():
                    for part in range(2):
                        push(
                            field.at[part, b], rbuf.at[b],
                            halo_send.at[side, part, b], relay_recv.at[b], via[part],
                        ).start()

            @pl.when(jnp.logical_not(edge & VIA_ONE))
            def _():
                for part in range(2):
                    halo_copy(side, part, b).start()
        return carry

    roles = ((0, low_at, relays_up, up_to), (1, high_at, relays_down, down_to))

    def relay_halo(b, carry):
        for side, at, role, to in roles:
            @pl.when(role)
            def _():
                pltpu.make_async_copy(rbuf.at[b], rbuf.at[b], relay_recv.at[b]).wait()
                push(
                    rbuf.at[b], vext.at[core, at + b],
                    relay_send.at[b], halo_recv.at[side, core, b], to,
                ).start()
        return carry

    lax.fori_loop(0, blocks, halo_start, 0)

    @pl.when(is_owner)
    def _():
        for way, go in both:
            @pl.when(go)
            def _():
                index_hop(way, index).start()
                energy_hop(way, energies).start()
        pltpu.make_async_copy(index, ibuf, index_recv).start()
        pltpu.make_async_copy(energies, ebuf, energy_recv).start()

        def send_piece(i, carry):
            for way, go in both:
                @pl.when(go)
                def _():
                    piece_hop(way, coupling, i).start()
            pltpu.make_async_copy(coupling.at[i], cbuf.at[i], couple_recv.at[i]).start()
            return carry

        lax.fori_loop(0, pieces, send_piece, 0)

    own = pltpu.make_async_copy(field, vext.at[:, pl.ds(blocks, blocks)], own_sem)
    own.start()

    pltpu.make_async_copy(ibuf, ibuf, index_recv).wait()
    pltpu.make_async_copy(ebuf, ebuf, energy_recv).wait()

    @pl.when(jnp.logical_not(is_owner))
    def _():
        for way, go in both:
            @pl.when(go)
            def _():
                index_hop(way, ibuf).start()
                energy_hop(way, ebuf).start()

    to_slots = pltpu.make_async_copy(ibuf, slots, slot_sem)
    to_slots.start()

    def take_pieces(first_piece, last_piece):
        def take(i, carry):
            pltpu.make_async_copy(cbuf.at[i], cbuf.at[i], couple_recv.at[i]).wait()

            @pl.when(jnp.logical_not(is_owner))
            def _():
                for way, go in both:
                    @pl.when(go)
                    def _():
                        piece_hop(way, cbuf, i).start()
            return carry

        lax.fori_loop(first_piece, last_piece, take, 0)

    def split_into(target, at, re, im):
        re_high, re_low = halves(re)
        im_high, im_low = halves(im)
        target[at, 0, :, 0:window] = re_high
        target[at, 0, :, window:] = im_high
        target[at, 1, :, 0:window] = re_low
        target[at, 1, :, window:] = im_low

    def product(r, source):
        total = [jnp.zeros((block, window), jnp.float32) for _ in range(2)]
        for k in range(0, width, 2):
            e0 = slots[0, r * width + k]
            e1 = slots[0, r * width + k + 1]
            lanes = pl.ds(k * block, 2 * block)
            high = chigh[r, :, lanes]
            low = clow[r, :, lanes]
            for part in range(2):
                span = pl.ds(part * window, window)
                v_high = jnp.concatenate([source[e0, 0, :, span], source[e1, 0, :, span]], axis=0)
                v_low = jnp.concatenate([source[e0, 1, :, span], source[e1, 1, :, span]], axis=0)
                total[part] += jnp.dot(high, v_high, preferred_element_type=jnp.float32)
                total[part] += jnp.dot(low, v_high, preferred_element_type=jnp.float32)
                total[part] += jnp.dot(high, v_low, preferred_element_type=jnp.float32)
        return total[0] * 0.125, total[1] * 0.125

    def next_copy(side, part, r):
        to, at = ((right, r), (left, high_at + r))[side]
        return push(
            wext.at[part, blocks + r], wext.at[part, at],
            next_send.at[side, part, r], next_recv.at[side, part, r], (to, col),
        )

    def next_start(side, r):
        edge, via = ((is_last, up_relay), (is_first, down_relay))[side]
        relayed_row = edge & (r < VIA_ROWS)

        @pl.when(relayed_row)
        def _():
            for part in range(2):
                push(
                    wext.at[part, blocks + r], sbuf.at[r],
                    next_send.at[side, part, r], relay_next_recv.at[r], via[part],
                ).start()

        @pl.when(jnp.logical_not(relayed_row))
        def _():
            for part in range(2):
                next_copy(side, part, r).start()

    def relay_next(r, carry):
        for side, at, role, to in roles:
            @pl.when(role)
            def _():
                pltpu.make_async_copy(sbuf.at[r], sbuf.at[r], relay_next_recv.at[r]).wait()
                push(
                    sbuf.at[r], wext.at[core, at + r],
                    relay_next_send.at[r], next_recv.at[side, core, r], to,
                ).start()
        return carry

    def first_row(r, carry):
        on_diagonal = lax.broadcasted_iota(jnp.int32, (block, block), 0) == lax.broadcasted_iota(
            jnp.int32, (block, block), 1
        )
        level = jnp.broadcast_to(ebuf[pl.ds(r, 1), :], (block, block))
        for k in range(width):
            value = cbuf[r * per_row + k // pair, k % pair]
            if k == 0:
                value = value + jnp.where(on_diagonal, level, 0.0)
            high, low = halves(value)
            chigh[r, :, k * block : (k + 1) * block] = high
            clow[r, :, k * block : (k + 1) * block] = low
        re, im = product(r, vhalf)
        wext[0, blocks + r] = re
        wext[1, blocks + r] = im
        split_into(whalf, blocks + r, re, im)
        next_start(0, r)
        next_start(1, r)
        return carry

    early = READY_ROWS * per_row
    passes_on = jnp.logical_not(is_owner) & (go_up | go_down)
    if VIA_ONE:
        @pl.when(jnp.logical_not(passes_on))
        def _():
            lax.fori_loop(0, blocks, relay_halo, 0)

    take_pieces(0, LEAD)
    if VIA_ONE:
        def pass_and_take(b, carry):
            @pl.when(passes_on)
            def _():
                relay_halo(b, 0)

            take_pieces(LEAD + b, LEAD + b + 1)
            return carry

        lax.fori_loop(0, blocks, pass_and_take, 0)
        take_pieces(LEAD + blocks, early)
    else:
        take_pieces(LEAD, early)

    own.wait()
    def halo_wait(b, carry):
        for side in range(2):
            for part in range(2):
                halo_copy(side, part, b).wait()
        return carry

    lax.fori_loop(0, blocks, halo_wait, 0)
    to_slots.wait()

    def split_field(e, carry):
        split_into(vhalf, e, vext[0, e], vext[1, e])
        return carry

    lax.fori_loop(0, 3 * blocks, split_field, 0)
    lax.fori_loop(0, READY_ROWS, first_row, 0)

    relayed_rows = list(range(VIA_ROWS))
    for r in range(READY_ROWS, blocks):
        take_pieces(r * per_row, (r + 1) * per_row)
        first_row(r, 0)
        for q in relayed_rows[:2]:
            relay_next(q, 0)
        relayed_rows = relayed_rows[2:]

    def split_next(r, carry):
        for side in range(2):
            for part in range(2):
                next_copy(side, part, r).wait()
        split_into(whalf, r, wext[0, r], wext[1, r])
        split_into(whalf, 2 * blocks + r, wext[0, 2 * blocks + r], wext[1, 2 * blocks + r])
        return carry

    lax.fori_loop(0, blocks, split_next, 0)
    cosine = phase[0]
    sine = phase[1]

    def last_row(r, carry):
        re, im = product(r, whalf)
        keep = bessel_zero + 2.0 * bessel_two
        u_re = keep * vext[0, blocks + r] + 2.0 * bessel_one * wext[1, blocks + r] - 4.0 * bessel_two * re
        u_im = keep * vext[1, blocks + r] - 2.0 * bessel_one * wext[0, blocks + r] - 4.0 * bessel_two * im
        out[0, r] = cosine * u_re + sine * u_im
        out[1, r] = cosine * u_im - sine * u_re
        return carry

    lax.fori_loop(0, blocks, last_row, 0)

    @pl.when(relays)
    def _():
        def drain_one(r, carry):
            push(rbuf.at[r], rbuf.at[r], relay_send.at[r], relay_recv.at[r], up_to).wait_send()
            return carry

        if VIA_ONE:
            lax.fori_loop(0, blocks, drain_one, 0)

        def drain_next(r, carry):
            push(sbuf.at[r], sbuf.at[r], relay_next_send.at[r], relay_next_recv.at[r], up_to).wait_send()
            return carry

        lax.fori_loop(0, VIA_ROWS, drain_next, 0)

    for way, go in both:
        @pl.when(go)
        def _():
            index_hop(way, ibuf).wait_send()
            energy_hop(way, ebuf).wait_send()

            def drain(i, carry):
                piece_hop(way, cbuf, i).wait_send()
                return carry

            lax.fori_loop(0, pieces, drain, 0)


def per_device(propagator, couplings, frame_energies, block_lists, frame_owner):
    line = lax.axis_size("cols")
    ring = lax.axis_size("space")
    moment = frame_owner[0]
    owner = jnp.mod(moment, line)
    turn = jnp.mod(moment // line, 97)
    _, blocks, width, block, _ = couplings.shape
    window = propagator.shape[2]
    angle = turn.astype(jnp.float32) * phase_unit
    phase = jnp.stack([jnp.cos(angle), jnp.sin(angle)])
    total_blocks = blocks * ring
    first_block = lax.axis_index("space") * blocks
    index = jnp.mod(block_lists[0] - first_block + REACH, total_blocks).astype(jnp.int32)
    index = jnp.pad(index.reshape(1, blocks * width), ((0, 7), (0, 128 - blocks * width)))
    energies = frame_energies.reshape(blocks, block)
    field = propagator.reshape(2, blocks, block, window)
    pieces = blocks * width // 2
    coupling = couplings.reshape(pieces, 2, block, block)

    def call(which):
        anywhere = pl.BlockSpec(memory_space=pl.ANY)
        dma = pltpu.SemaphoreType.DMA
        return pl.pallas_call(
            functools.partial(step_kernel, which, ring, line, blocks, width, block, window),
            out_shape=jax.ShapeDtypeStruct((2, blocks, block, window), jnp.float32),
            in_specs=[pl.BlockSpec(memory_space=pltpu.SMEM)] + [anywhere] * 4,
            out_specs=pl.BlockSpec(memory_space=pltpu.VMEM),
            scratch_shapes=[
                pltpu.VMEM((2, 3 * blocks, block, window), jnp.float32),
                pltpu.VMEM((2, 3 * blocks, block, window), jnp.float32),
                pltpu.VMEM((3 * blocks, 2, block, 2 * window), jnp.bfloat16),
                pltpu.VMEM((3 * blocks, 2, block, 2 * window), jnp.bfloat16),
                pltpu.VMEM((pieces, 2, block, block), jnp.float32),
                pltpu.VMEM((blocks, block, width * block), jnp.bfloat16),
                pltpu.VMEM((blocks, block, width * block), jnp.bfloat16),
                pltpu.VMEM((blocks, block), jnp.float32),
                pltpu.VMEM((8, 128), jnp.int32),
                pltpu.SMEM((8, 128), jnp.int32),
                dma((2, 2, blocks)), dma((2, 2, blocks)), dma,
                dma((2, 2, blocks)), dma((2, 2, blocks)),
                dma((2, pieces)), dma((pieces,)),
                dma((2,)), dma, dma((2,)), dma, dma,
                pltpu.VMEM((blocks, block, window), jnp.float32),
                pltpu.VMEM((blocks, block, window), jnp.float32),
                dma((blocks,)), dma((blocks,)), dma((blocks,)), dma((blocks,)),
            ],
            compiler_params=pltpu.CompilerParams(
                collective_id=which, has_side_effects=True, vmem_limit_bytes=48 << 20
            ),
            name="step",
        )

    branches = [call(which) for which in range(line)]
    result = lax.switch(owner, branches, phase, energies, index, field, coupling)
    return result.reshape(2, blocks * block, window)


def solution(mesh):
    in_specs = (
        P(None, "space", "cols"),
        P("cols", "space", None, None, None),
        P("cols", "space"),
        P("cols", "space", None),
        P(),
    )
    out_specs = P(None, "space", "cols")
    return jax.shard_map(
        per_device, mesh=mesh, in_specs=in_specs, out_specs=out_specs, check_vma=False
    )
```
